32 devices in a mesh: grp: 4 (over z), gx: 2 (over y), gy: 4 (over x, core).
Axes of the slice: x: 2, y: 2, z: 4, core: 2. Of those that a mesh axis runs over, the one named last changes fastest.
Arguments:
- checkpoint: float32 [2, 2, 2, 32, 64, 256], P(None, None, None, 'gx', 'gy'), may hold values from -6 to 6
- courant: float32 [32, 64, 256], P('gx', 'gy'), may hold values from 0.03 to 0.15
- epsilon: float32 [32, 64, 256], P('gx', 'gy'), may hold values from 0.3 to 0.6
- delta: float32 [32, 64, 256], P('gx', 'gy'), may hold values from 0.05 to 0.3
- positions: int32 [4, 3, 512], replicated, may hold values from 0 to 255, as said below
- amplitudes: float32 [4, 16, 512], replicated, may hold values from -6 to 6
- offsets: int32 [16], replicated, may hold values from -8 to 8, as said below
Outputs:
- image: float32 [16, 32, 64, 256], P('grp', 'gx', 'gy')
The draws below stay inside these ranges and needn't reach their ends.
Inputs may be any that keep to these rules, and one draw needn't show every extreme that they name: `positions`: each column of a row is a cell inside the grid: x below 32, y below 64, z below 256. `offsets`: both -8 and 8 occur.
All inputs are finite; a program needn't handle non-finite values.
Results may differ from the reference program's by a relative error of at most 0.0003.
Values sent between devices are 32-bit elements; how exact they have to be, the bound alone decides.
A program may use at most 128 MiB of HBM per device.

```python
import math
import jax
import jax.numpy as jnp
from jax import lax

NZ = 256
NREC = 512
NSTEPS = 16
SNAP = 4
HMAX = 8
NH = 16
GROUPS = 4
SHOTS = 2
NX = 32
NY = 64


def draw_positions(key, part):
    key_x, key_y, key_z = jax.random.split(jax.random.fold_in(key, 11), 3)
    shape = (GROUPS, NREC)
    coord_x = jax.random.randint(key_x, shape, 0, NX)
    coord_y = jax.random.randint(key_y, shape, 0, NY)
    coord_z = jax.random.randint(key_z, shape, 0, NZ)
    return jnp.stack([coord_x, coord_y, coord_z], 1).astype(jnp.int32)


def draw_offsets(key, part):
    key_vals, key_perm = jax.random.split(jax.random.fold_in(key, 23))
    values = jax.random.randint(key_vals, (NH,), -HMAX, HMAX + 1)
    order = jax.random.permutation(key_perm, NH)
    values = values.at[order[0]].set(HMAX).at[order[1]].set(-HMAX)
    return values.astype(jnp.int32)


def levels(rng, dims, cuts, low, high):
    level, own = 1.0, jax.random.fold_in(rng, 6)
    for dim, parts in cuts:
        steps = jnp.exp(jax.random.uniform(jax.random.fold_in(own, dim), (parts,), jnp.float32, low / len(cuts), high / len(cuts)))
        level = level * jnp.repeat(steps, dims[dim] // parts).reshape([-1 if axis == dim else 1 for axis in range(len(dims))])
    return level


def noise(own_key, dims, width, limit, cuts=(), dtype=jnp.bfloat16):
    factor_of = levels(own_key, dims, cuts, -0.22, 0.18) if cuts else 1.0
    entries = jax.random.normal(own_key, dims, jnp.float32) * width * factor_of
    return jnp.minimum(jnp.maximum(entries, -limit), limit).astype(dtype)


def setup_inputs(seed: int = 0) -> dict:
    streams_of = jax.random.split(jax.random.key(seed), 8)
    checkpoint = noise(streams_of[0], (SHOTS, 2, 2, NX, NY, NZ), 1.0, 6.0, ((3, 2), (4, 4)), jnp.float32)
    courant = jnp.clip(jnp.exp(math.log(0.15) - 1.609438 * jax.random.uniform(streams_of[1], (NX, NY, NZ), jnp.float32) ** levels(streams_of[1], (NX, NY, NZ), ((0, 2), (1, 4)), -0.2, 0.2)), 0.03, 0.15)
    epsilon = jnp.clip(0.3 + 0.3 * jax.random.uniform(streams_of[2], (NX, NY, NZ), jnp.float32) ** levels(streams_of[2], (NX, NY, NZ), ((0, 2), (1, 4)), -0.2, 0.2), 0.3, 0.6)
    delta = jnp.clip(0.05 + 0.25 * jax.random.uniform(streams_of[3], (NX, NY, NZ), jnp.float32) ** levels(streams_of[3], (NX, NY, NZ), ((0, 2), (1, 4)), -0.2, 0.2), 0.05, 0.3)
    positions = draw_positions(jax.random.fold_in(streams_of[7], 71), 0)
    amplitudes = noise(streams_of[5], (GROUPS, NSTEPS, NREC), 1.0, 6.0, (), jnp.float32)
    offsets = draw_offsets(jax.random.fold_in(streams_of[7], 71), 0)
    return dict(checkpoint=checkpoint, courant=courant, epsilon=epsilon, delta=delta, positions=positions, amplitudes=amplitudes, offsets=offsets)


def laplacians(main_field, aux_field):
    padded = jnp.pad(main_field, ((1, 1), (1, 1), (0, 0)))
    across = padded[2:, 1:-1] + padded[:-2, 1:-1] + padded[1:-1, 2:] + padded[1:-1, :-2] - 4.0 * main_field
    deep_pad = jnp.pad(aux_field, ((0, 0), (0, 0), (1, 1)))
    vertical = deep_pad[:, :, 2:] + deep_pad[:, :, :-2] - 2.0 * aux_field
    return (across, vertical)

def replay(current, previous, coefs, coords, strengths):
    flat_index = ((coords[0] * NY + coords[1]) * NZ + coords[2]).astype(jnp.int32)
    snapshots = []
    for moment in range(NSTEPS):
        across, vertical = laplacians(current[0], current[1])
        source = jnp.zeros((NX * NY * NZ,), jnp.float32).at[flat_index].add(strengths[moment]).reshape(NX, NY, NZ)
        main_next = 2.0 * current[0] - previous[0] + coefs[0] * across + coefs[1] * vertical + source
        aux_next = 2.0 * current[1] - previous[1] + coefs[1] * across + coefs[2] * vertical + source
        previous = current
        current = jnp.stack([main_next, aux_next])
        if (moment + 1) % SNAP == 0:
            snapshots.append(current[0])
    return snapshots

def reference(checkpoint, courant, epsilon, delta, positions, amplitudes, offsets):
    coefs = jnp.stack([courant + 2.0 * courant * epsilon, courant * jnp.sqrt(2.0 * delta + 1.0), courant])
    zero_state = jnp.zeros_like(checkpoint[0, 0])
    pairs = []
    for shot in range(SHOTS):
        source_snaps = replay(checkpoint[shot, 0], checkpoint[shot, 1], coefs, positions[2 * shot], amplitudes[2 * shot])
        receiver_snaps = replay(zero_state, zero_state, coefs, positions[2 * shot + 1], amplitudes[2 * shot + 1])
        pairs.append((source_snaps, receiver_snaps))
    margins = ((HMAX, HMAX), (0, 0), (0, 0))

    def one_offset(shift):
        total = jnp.zeros((NX, NY, NZ), jnp.float32)
        for source_snaps, receiver_snaps in pairs:
            for number in range(len(source_snaps)):
                padded_source = jnp.pad(source_snaps[number], margins)
                shifted_source = lax.dynamic_slice_in_dim(padded_source, (HMAX - shift).astype(jnp.int32), NX, 0)
                padded_recv = jnp.pad(receiver_snaps[number], margins)
                shifted_recv = lax.dynamic_slice_in_dim(padded_recv, (HMAX + shift).astype(jnp.int32), NX, 0)
                total = total + shifted_source * shifted_recv
        return total
    return lax.map(one_offset, offsets)
```

```python
import functools
import jax
import jax.numpy as jnp
from jax import lax
from jax.experimental import pallas as pl
from jax.experimental.pallas import tpu as pltpu
from jax.sharding import PartitionSpec as P

SNAP = 4
HMAX = 8
MESH = pl.DeviceIdType.MESH


def kernel(sizes, courant, epsilon, delta, checkpoint, positions, amplitudes, offsets, out,
           state, hor, cpl, ver, inj, pick, spot, snaps, image, outgoing, gathered, hx, hy, sy,
           hs, hr, ss, sr, gs, gr):
    ng, nx, ny = sizes
    shots = checkpoint.shape[0]
    tx, ty, nz = courant.shape
    nrec = positions.shape[2]
    blocks = amplitudes.shape[1] // SNAP
    nh = offsets.shape[0]
    own = nh // ng
    qy = ty // ng
    sub = shots * qy
    groups = tx // qy
    g, a, b = lax.axis_index("grp"), lax.axis_index("gx"), lax.axis_index("gy")
    flip = b % 2
    sign = 1 - 2 * flip
    q = g + flip * (ng - 1 - 2 * g)

    inner_lo, inner_hi = (q > 0).astype(jnp.int32), (q < ng - 1).astype(jnp.int32)
    sides = (
        (a > 0, {"grp": g, "gx": a - 1, "gy": b}),
        (a < nx - 1, {"grp": g, "gx": a + 1, "gy": b}),
        ((q > 0) | (b > 0), {"grp": g - sign * inner_lo, "gx": a, "gy": b - 1 + inner_lo}),
        ((q < ng - 1) | (b < ny - 1), {"grp": g + sign * inner_hi, "gx": a, "gy": b + 1 - inner_hi}),
    )

    barrier = pltpu.get_barrier_semaphore()
    for there, device in sides:
        @pl.when(there)
        def _(device=device):
            pl.semaphore_signal(barrier, inc=1, device_id=device, device_id_type=MESH)
    for step in range(1, ng):
        pl.semaphore_signal(
            barrier, inc=1, device_id={"grp": (g + step) % ng, "gx": a, "gy": b}, device_id_type=MESH
        )

    rows = lax.broadcasted_iota(jnp.int32, (sub, nz), 0)
    lanes = lax.broadcasted_iota(jnp.int32, (sub, nz), 1)
    place = rows % qy
    is_odd = rows * 0 + q % 2 == 1
    first = rows < qy
    half = pl.ds(pl.multiple_of((q // 2) * sub, sub), sub)

    def turn(v, shift, axis=0):
        shift = shift % v.shape[axis]
        return v if shift == 0 else pltpu.roll(v, shift, axis)

    def low(v):
        return jnp.where(is_odd, turn(v, qy), v)

    def high(v):
        return jnp.where(is_odd, v, turn(v, qy))

    def both(v):
        return jnp.where(first, low(v), high(v))

    zero = jnp.zeros((sub, nz), jnp.float32)

    def prepare(x, carry):
        c, e, d = both(courant[x, half, :]), both(epsilon[x, half, :]), both(delta[x, half, :])
        hor[x] = c + 2.0 * c * e
        cpl[x] = c * jnp.sqrt(2.0 * d + 1.0)
        ver[x] = c
        for moment in range(2):
            for field in range(2):
                state[moment, field, 0, x] = jnp.where(
                    first, low(checkpoint[0, moment, field, x, half, :]), high(checkpoint[1, moment, field, x, half, :])
                )
                state[moment, field, 1, x] = zero
        return carry

    lax.fori_loop(0, tx, prepare, 0)

    def pack(side, r, slot, source):
        for m in range(groups):
            packed = None
            for i in range(qy):
                tile = turn(source(m * qy + i), i if side == 0 else i - (qy - 1))
                packed = tile if packed is None else jnp.where(place == i, tile, packed)
            sy[slot, side, r, m] = packed

    for r in range(2):
        for side in range(2):
            pack(side, r, 0, lambda x: state[0, 0, r, x])

    for side in range(2):
        for slot in range(2):
            @pl.when(jnp.logical_not(sides[side][0]))
            def _(slot=slot, side=side):
                hx[slot, side] = jnp.zeros(hx.shape[2:], jnp.float32)

            @pl.when(jnp.logical_not(sides[2 + side][0]))
            def _(slot=slot, side=side):
                hy[slot, side] = jnp.zeros(hy.shape[2:], jnp.float32)

    total = ng - 1
    for there, _ in sides:
        total = total + there.astype(jnp.int32)
    pl.semaphore_wait(barrier, total)

    def halo_copy(slot, side):
        if side < 2:
            source, target = state.at[slot, 0, :, 0 if side == 0 else tx - 1], hx.at[slot, 1 - side]
        else:
            source, target = sy.at[slot, side - 2], hy.at[slot, 3 - side]
        return pltpu.make_async_remote_copy(
            src_ref=source, dst_ref=target, send_sem=hs.at[slot, side], recv_sem=hr.at[slot, side ^ 1],
            device_id=sides[side][1], device_id_type=MESH,
        )

    def halo_arrival(slot, side):
        target = hx.at[slot, side] if side < 2 else hy.at[slot, side - 2]
        return pltpu.make_async_remote_copy(
            src_ref=target, dst_ref=target, send_sem=hs.at[slot, side], recv_sem=hr.at[slot, side],
            device_id=sides[side][1], device_id_type=MESH,
        )

    def snap_copy(j, side, arrival=False):
        source = pl.ds(HMAX, HMAX) if side == 0 else pl.ds(tx, HMAX)
        target = pl.ds(HMAX + tx, HMAX) if side == 0 else pl.ds(0, HMAX)
        if arrival:
            source = target = pl.ds(0, HMAX) if side == 0 else pl.ds(HMAX + tx, HMAX)
        return pltpu.make_async_remote_copy(
            src_ref=snaps.at[j, :, source], dst_ref=snaps.at[j, :, target], send_sem=ss.at[j, side],
            recv_sem=sr.at[j, side if arrival else side ^ 1], device_id=sides[side][1], device_id_type=MESH,
        )

    def send_halos(slot):
        for side in (2, 3, 0, 1):
            @pl.when(sides[side][0])
            def _(side=side):
                halo_copy(slot, side).start()

    def wait_halos(slot):
        for side in range(4):
            @pl.when(sides[side][0])
            def _(side=side):
                halo_arrival(slot, side).wait_recv()
                halo_copy(slot, side).wait_send()

    def send_snap(j):
        for side in range(2):
            @pl.when(sides[side][0])
            def _(side=side):
                snap_copy(j, side).start()

    def wait_snap(j):
        for side in range(2):
            @pl.when(sides[side][0])
            def _(side=side):
                snap_copy(j, side, True).wait_recv()
                snap_copy(j, side).wait_send()

    send_halos(0)

    column = lax.broadcasted_iota(jnp.int32, (tx * sub, nrec), 0)
    level = lax.broadcasted_iota(jnp.int32, (nz, nrec), 0)
    for r in range(2):
        for s in range(shots):
            px = positions[2 * s + r, 0:1, :] - a * tx
            py = positions[2 * s + r, 1:2, :] - (b * ty + q * qy)
            pz = positions[2 * s + r, 2:3, :]
            inside = (px >= 0) & (px < tx) & (py >= 0) & (py < qy)
            cell = jnp.where(inside, px * sub + s * qy + py, -1)
            points = pl.ds(s * nrec, nrec)
            pick[r, :, points] = jnp.where(column == cell, 1.0, 0.0)
            spot[r, points, :] = jnp.where(level == pz, 1.0, 0.0).T.astype(jnp.bfloat16)

    def clear(k, carry):
        for x in range(tx):
            image[k, x] = zero
        return carry

    lax.fori_loop(0, nh, clear, 0)
    for side in range(2):
        @pl.when(jnp.logical_not(sides[side][0]))
        def _(side=side):
            def blank(j, carry):
                for r in range(2):
                    for x in range(HMAX):
                        snaps[j, r, side * (HMAX + tx) + x] = zero
                return carry

            lax.fori_loop(0, blocks, blank, 0)

    def inject(moment):
        for r in range(2):
            found = None
            for s in range(shots):
                points = pl.ds(s * nrec, nrec)
                strength = amplitudes[2 * s + r, pl.ds(moment, 1), :]
                spread = pick[r, :, points] * strength
                upper = spread.astype(jnp.bfloat16)
                lower = (spread - upper.astype(jnp.float32)).astype(jnp.bfloat16)
                for part in (upper, lower):
                    term = jnp.dot(part, spot[r, points, :], preferred_element_type=jnp.float32)
                    found = term if found is None else found + term
            inj[r] = found

    def advance(p):
        for r in range(2):
            for x in range(tx):
                m, w = state[p, 0, r, x], state[p, 1, r, x]
                across = (
                    jnp.where(place == 0, 0.0, turn(m, 1))
                    + jnp.where(place == qy - 1, 0.0, turn(m, -1))
                    - 4.0 * m
                )
                if x > 0:
                    across = across + state[p, 0, r, x - 1]
                if x < tx - 1:
                    across = across + state[p, 0, r, x + 1]
                down = (
                    jnp.where(lanes == 0, 0.0, turn(w, 1, 1))
                    + jnp.where(lanes == nz - 1, 0.0, turn(w, -1, 1))
                    - 2.0 * w
                )
                source = inj[r, pl.ds(x * sub, sub), :]
                coupling = cpl[x]
                state[1 - p, 0, r, x] = 2.0 * m - state[1 - p, 0, r, x] + hor[x] * across + coupling * down + source
                state[1 - p, 1, r, x] = 2.0 * w - state[1 - p, 1, r, x] + coupling * across + ver[x] * down + source

    def repair(p, j):
        for r in range(2):
            for m in range(groups):
                below, above = hy[p, 0, r, m], hy[p, 1, r, m]
                packed = [None, None]
                for i in range(qy):
                    x = m * qy + i
                    extra = jnp.where(place == 0, turn(below, -i), 0.0)
                    extra = jnp.where(place == qy - 1, turn(above, qy - 1 - i), extra)
                    if x == 0:
                        extra = extra + hx[p, 0, r]
                    if x == tx - 1:
                        extra = extra + hx[p, 1, r]
                    main = state[1 - p, 0, r, x] + hor[x] * extra
                    state[1 - p, 0, r, x] = main
                    state[1 - p, 1, r, x] = state[1 - p, 1, r, x] + cpl[x] * extra
                    for side in range(2):
                        tile = turn(main, i if side == 0 else i - (qy - 1))
                        packed[side] = tile if i == 0 else jnp.where(place == i, tile, packed[side])
                    if j is not None:
                        snaps[j, r, HMAX + x] = main
                for side in range(2):
                    sy[1 - p, side, r, m] = packed[side]

    def correlate(j):
        def one(k, carry):
            shift = offsets[k]
            for x in range(tx):
                image[k, x] = image[k, x] + snaps[j, 0, HMAX - shift + x] * snaps[j, 1, HMAX + shift + x]
            return carry

        lax.fori_loop(0, nh, one, 0)

    def block(j, carry):
        for i in range(SNAP):
            p = i % 2
            if i == 0:
                @pl.when(j > 0)
                def _():
                    send_halos(p)
                    send_snap(j - 1)
            else:
                send_halos(p)
            inject(j * SNAP + i)
            advance(p)
            if i == 2:
                @pl.when(j > 0)
                def _():
                    wait_snap(j - 1)
                    correlate(j - 1)
            wait_halos(p)
            repair(p, j if i == SNAP - 1 else None)
        return carry

    lax.fori_loop(0, blocks, block, 0)
    send_snap(blocks - 1)
    wait_snap(blocks - 1)

    def peer_copy(d, arrival=False):
        return pltpu.make_async_remote_copy(
            src_ref=outgoing.at[d], dst_ref=gathered.at[d if arrival else g], send_sem=gs.at[d],
            recv_sem=gr.at[d if arrival else g],
            device_id={"grp": d, "gx": a, "gy": b}, device_id_type=MESH,
        )

    def finish(d, target):
        def pair(n, carry):
            for x in range(tx):
                tiles = []
                for c in range(2):
                    k = d * own + 2 * n + c
                    shift = offsets[k]
                    tile = image[k, x] + snaps[blocks - 1, 0, HMAX - shift + x] * snaps[blocks - 1, 1, HMAX + shift + x]
                    tiles.append(tile + turn(tile, qy))
                target[n, x] = jnp.where(first, tiles[0], tiles[1])
            return carry

        lax.fori_loop(0, own // 2, pair, 0)

    for step in range(1, ng):
        d = (g + step) % ng
        finish(d, outgoing.at[d])
        peer_copy(d).start()
    finish(g, gathered.at[g])
    for step in range(1, ng):
        d = (g + step) % ng
        peer_copy(d, True).wait_recv()
        peer_copy(d).wait_send()

    def place_out(x, carry):
        for h in range(ng // 2):
            left, right = 2 * h, 2 * h + 1
            one = left + flip * (ng - 1 - 2 * left)
            two = right + flip * (ng - 1 - 2 * right)
            for n in range(own // 2):
                u, v = gathered[one, n, x], gathered[two, n, x]
                out[2 * n, x, pl.ds(h * sub, sub), :] = jnp.where(first, u, turn(v, qy))
                out[2 * n + 1, x, pl.ds(h * sub, sub), :] = jnp.where(first, turn(u, qy), v)
        return carry

    lax.fori_loop(0, tx, place_out, 0)


def shards(sizes, checkpoint, courant, epsilon, delta, positions, amplitudes, offsets):
    ng, nx, ny = sizes
    shots = checkpoint.shape[0]
    tx, ty, nz = courant.shape
    nrec = positions.shape[2]
    blocks = amplitudes.shape[1] // SNAP
    nh = offsets.shape[0]
    own = nh // ng
    qy = ty // ng
    sub = shots * qy
    groups = tx // qy
    assert shots == 2 and sub == 8 and ng % 2 == 0 and own % 2 == 0 and tx % qy == 0 and tx >= HMAX
    f32 = jnp.float32
    dma = pltpu.SemaphoreType.DMA
    vmem = pl.BlockSpec(memory_space=pltpu.VMEM)
    return pl.pallas_call(
        functools.partial(kernel, sizes),
        out_shape=jax.ShapeDtypeStruct((own, tx, ty, nz), f32),
        in_specs=[vmem] * 6 + [pl.BlockSpec(memory_space=pltpu.SMEM)],
        out_specs=vmem,
        scratch_shapes=[
            pltpu.VMEM((2, 2, 2, tx, sub, nz), f32),
            pltpu.VMEM((tx, sub, nz), f32),
            pltpu.VMEM((tx, sub, nz), f32),
            pltpu.VMEM((tx, sub, nz), f32),
            pltpu.VMEM((2, tx * sub, nz), f32),
            pltpu.VMEM((2, tx * sub, shots * nrec), f32),
            pltpu.VMEM((2, shots * nrec, nz), jnp.bfloat16),
            pltpu.VMEM((blocks, 2, tx + 2 * HMAX, sub, nz), f32),
            pltpu.VMEM((nh, tx, sub, nz), f32),
            pltpu.VMEM((ng, own // 2, tx, sub, nz), f32),
            pltpu.VMEM((ng, own // 2, tx, sub, nz), f32),
            pltpu.VMEM((2, 2, 2, sub, nz), f32),
            pltpu.VMEM((2, 2, 2, groups, sub, nz), f32),
            pltpu.VMEM((2, 2, 2, groups, sub, nz), f32),
            dma((2, 4)),
            dma((2, 4)),
            dma((blocks, 2)),
            dma((blocks, 2)),
            dma((ng,)),
            dma((ng,)),
        ],
        compiler_params=pltpu.CompilerParams(
            collective_id=0, has_side_effects=True, vmem_limit_bytes=56 * 1024 * 1024
        ),
    )(courant, epsilon, delta, checkpoint, positions, amplitudes, offsets)


def solution(mesh):
    sizes = tuple(mesh.shape[axis] for axis in ("grp", "gx", "gy"))
    return jax.shard_map(
        functools.partial(shards, sizes),
        mesh=mesh,
        in_specs=(
            P(None, None, None, "gx", "gy", None),
            P("gx", "gy", None),
            P("gx", "gy", None),
            P("gx", "gy", None),
            P(),
            P(),
            P(),
        ),
        out_specs=P("grp", "gx", "gy", None),
        check_vma=False,
    )
```

```python
import functools
import math
import jax
import jax.numpy as jnp
from jax import lax
from jax.experimental import pallas as pl
from jax.experimental.pallas import tpu as pltpu
from jax.sharding import PartitionSpec as P

SNAP = 4
HMAX = 8
MESH = pl.DeviceIdType.MESH


def kernel(sizes, courant, epsilon, delta, checkpoint, positions, amplitudes, offsets, gathered,
           state, hor, cpl, ver, inj, pick, spot, snaps, image, outgoing, hx, hy, sy,
           hs, hr, ss, sr, gs, gr):
    ng, nx, ny = sizes
    shots = checkpoint.shape[0]
    tx, ty, nz = courant.shape
    nrec = positions.shape[2]
    blocks = amplitudes.shape[1] // SNAP
    nh = offsets.shape[0]
    own = nh // ng
    qy = ty // ng
    sub = shots * qy
    groups = tx // qy
    g, a, b = lax.axis_index("grp"), lax.axis_index("gx"), lax.axis_index("gy")
    flip = b % 2
    sign = 1 - 2 * flip
    q = g + flip * (ng - 1 - 2 * g)

    inner_lo, inner_hi = (q > 0).astype(jnp.int32), (q < ng - 1).astype(jnp.int32)
    sides = (
        (a > 0, {"grp": g, "gx": a - 1, "gy": b}),
        (a < nx - 1, {"grp": g, "gx": a + 1, "gy": b}),
        ((q > 0) | (b > 0), {"grp": g - sign * inner_lo, "gx": a, "gy": b - 1 + inner_lo}),
        ((q < ng - 1) | (b < ny - 1), {"grp": g + sign * inner_hi, "gx": a, "gy": b + 1 - inner_hi}),
    )

    barrier = pltpu.get_barrier_semaphore()
    for there, device in sides:
        @pl.when(there)
        def _(device=device):
            pl.semaphore_signal(barrier, inc=1, device_id=device, device_id_type=MESH)
    for step in range(1, ng):
        pl.semaphore_signal(
            barrier, inc=1, device_id={"grp": (g + step) % ng, "gx": a, "gy": b}, device_id_type=MESH
        )

    rows = lax.broadcasted_iota(jnp.int32, (sub, nz), 0)
    lanes = lax.broadcasted_iota(jnp.int32, (sub, nz), 1)
    place = rows % qy
    is_odd = rows * 0 + q % 2 == 1
    first = rows < qy
    half = pl.ds(pl.multiple_of((q // 2) * sub, sub), sub)

    def turn(v, shift, axis=0):
        shift = shift % v.shape[axis]
        return v if shift == 0 else pltpu.roll(v, shift, axis)

    def low(v):
        return jnp.where(is_odd, turn(v, qy), v)

    def high(v):
        return jnp.where(is_odd, v, turn(v, qy))

    def both(v):
        return jnp.where(first, low(v), high(v))

    zero = jnp.zeros((sub, nz), jnp.float32)

    def prepare(x, carry):
        c, e, d = both(courant[x, half, :]), both(epsilon[x, half, :]), both(delta[x, half, :])
        hor[x] = c + 2.0 * c * e
        cpl[x] = c * jnp.sqrt(2.0 * d + 1.0)
        ver[x] = c
        for moment in range(2):
            for field in range(2):
                state[moment, field, 0, x] = jnp.where(
                    first, low(checkpoint[0, moment, field, x, half, :]), high(checkpoint[1, moment, field, x, half, :])
                )
                state[moment, field, 1, x] = zero
        return carry

    lax.fori_loop(0, tx, prepare, 0)

    def pack(side, r, slot, source):
        for m in range(groups):
            packed = None
            for i in range(qy):
                tile = turn(source(m * qy + i), i if side == 0 else i - (qy - 1))
                packed = tile if packed is None else jnp.where(place == i, tile, packed)
            sy[slot, side, r, m] = packed

    for r in range(2):
        for side in range(2):
            pack(side, r, 0, lambda x: state[0, 0, r, x])

    for side in range(2):
        for slot in range(2):
            @pl.when(jnp.logical_not(sides[side][0]))
            def _(slot=slot, side=side):
                hx[slot, side] = jnp.zeros(hx.shape[2:], jnp.float32)

            @pl.when(jnp.logical_not(sides[2 + side][0]))
            def _(slot=slot, side=side):
                hy[slot, side] = jnp.zeros(hy.shape[2:], jnp.float32)

    total = ng - 1
    for there, _ in sides:
        total = total + there.astype(jnp.int32)
    pl.semaphore_wait(barrier, total)

    def halo_copy(slot, r, side):
        if side < 2:
            source, target = state.at[slot, 0, r, 0 if side == 0 else tx - 1], hx.at[slot, 1 - side, r]
        else:
            source, target = sy.at[slot, side - 2, r], hy.at[slot, 3 - side, r]
        return pltpu.make_async_remote_copy(
            src_ref=source, dst_ref=target, send_sem=hs.at[slot, r, side], recv_sem=hr.at[slot, r, side ^ 1],
            device_id=sides[side][1], device_id_type=MESH,
        )

    def halo_arrival(slot, r, side):
        target = hx.at[slot, side, r] if side < 2 else hy.at[slot, side - 2, r]
        return pltpu.make_async_remote_copy(
            src_ref=target, dst_ref=target, send_sem=hs.at[slot, r, side], recv_sem=hr.at[slot, r, side],
            device_id=sides[side][1], device_id_type=MESH,
        )

    def snap_copy(j, r, side, arrival=False):
        source = pl.ds(HMAX, HMAX) if side == 0 else pl.ds(tx, HMAX)
        target = pl.ds(HMAX + tx, HMAX) if side == 0 else pl.ds(0, HMAX)
        if arrival:
            source = target = pl.ds(0, HMAX) if side == 0 else pl.ds(HMAX + tx, HMAX)
        return pltpu.make_async_remote_copy(
            src_ref=snaps.at[j, r, source], dst_ref=snaps.at[j, r, target], send_sem=ss.at[j, r, side],
            recv_sem=sr.at[j, r, side if arrival else side ^ 1], device_id=sides[side][1], device_id_type=MESH,
        )

    def send_halos(slot, r):
        for side in (2, 3, 0, 1):
            @pl.when(sides[side][0])
            def _(side=side):
                halo_copy(slot, r, side).start()

    def wait_halos(slot, r):
        for side in range(4):
            @pl.when(sides[side][0])
            def _(side=side):
                halo_arrival(slot, r, side).wait_recv()
                halo_copy(slot, r, side).wait_send()

    def send_snap(j, r):
        for side in range(2):
            @pl.when(sides[side][0])
            def _(side=side):
                snap_copy(j, r, side).start()

    def wait_snap(j):
        for r in range(2):
            for side in range(2):
                @pl.when(sides[side][0])
                def _(r=r, side=side):
                    snap_copy(j, r, side, True).wait_recv()
                    snap_copy(j, r, side).wait_send()

    send_halos(0, 0)
    send_halos(0, 1)

    column = lax.broadcasted_iota(jnp.int32, (tx * sub, nrec), 0)
    level = lax.broadcasted_iota(jnp.int32, (nz, nrec), 0)
    for r in range(2):
        for s in range(shots):
            px = positions[0, 2 * s + r : 2 * s + r + 1, :] - a * tx
            py = positions[1, 2 * s + r : 2 * s + r + 1, :] - (b * ty + q * qy)
            pz = positions[2, 2 * s + r : 2 * s + r + 1, :]
            inside = (px >= 0) & (px < tx) & (py >= 0) & (py < qy)
            cell = jnp.where(inside, px * sub + s * qy + py, -1)
            points = pl.ds(s * nrec, nrec)
            pick[r, :, points] = jnp.where(column == cell, 1.0, 0.0)
            spot[r, points, :] = jnp.where(level == pz, 1.0, 0.0).T.astype(jnp.bfloat16)

    def clear(k, carry):
        for x in range(tx):
            image[k, x] = zero
        return carry

    lax.fori_loop(0, nh, clear, 0)
    for side in range(2):
        @pl.when(jnp.logical_not(sides[side][0]))
        def _(side=side):
            def blank(j, carry):
                for r in range(2):
                    for x in range(HMAX):
                        snaps[j, r, side * (HMAX + tx) + x] = zero
                return carry

            lax.fori_loop(0, blocks, blank, 0)

    def inject(moment, r):
        found = None
        for s in range(shots):
            points = pl.ds(s * nrec, nrec)
            strength = amplitudes[2 * s + r, pl.ds(moment, 1), :]
            spread = pick[r, :, points] * strength
            upper = spread.astype(jnp.bfloat16)
            lower = (spread - upper.astype(jnp.float32)).astype(jnp.bfloat16)
            for part in (upper, lower):
                term = jnp.dot(part, spot[r, points, :], preferred_element_type=jnp.float32)
                found = term if found is None else found + term
        inj[r] = found

    def advance(p, r):
        for x in range(tx):
            m, w = state[p, 0, r, x], state[p, 1, r, x]
            across = (
                jnp.where(place == 0, 0.0, turn(m, 1))
                + jnp.where(place == qy - 1, 0.0, turn(m, -1))
                - 4.0 * m
            )
            if x > 0:
                across = across + state[p, 0, r, x - 1]
            if x < tx - 1:
                across = across + state[p, 0, r, x + 1]
            down = (
                jnp.where(lanes == 0, 0.0, turn(w, 1, 1))
                + jnp.where(lanes == nz - 1, 0.0, turn(w, -1, 1))
                - 2.0 * w
            )
            source = inj[r, pl.ds(x * sub, sub), :]
            coupling = cpl[x]
            state[1 - p, 0, r, x] = 2.0 * m - state[1 - p, 0, r, x] + hor[x] * across + coupling * down + source
            state[1 - p, 1, r, x] = 2.0 * w - state[1 - p, 1, r, x] + coupling * across + ver[x] * down + source

    def repair(p, r, j):
        for m in range(groups):
            below, above = hy[p, 0, r, m], hy[p, 1, r, m]
            packed = [None, None]
            for i in range(qy):
                x = m * qy + i
                extra = jnp.where(place == 0, turn(below, -i), 0.0)
                extra = jnp.where(place == qy - 1, turn(above, qy - 1 - i), extra)
                if x == 0:
                    extra = extra + hx[p, 0, r]
                if x == tx - 1:
                    extra = extra + hx[p, 1, r]
                main = state[1 - p, 0, r, x] + hor[x] * extra
                state[1 - p, 0, r, x] = main
                state[1 - p, 1, r, x] = state[1 - p, 1, r, x] + cpl[x] * extra
                for side in range(2):
                    tile = turn(main, i if side == 0 else i - (qy - 1))
                    packed[side] = tile if i == 0 else jnp.where(place == i, tile, packed[side])
                if j is not None:
                    snaps[j, r, HMAX + x] = main
            for side in range(2):
                sy[1 - p, side, r, m] = packed[side]

    def correlate(j):
        def one(k, carry):
            shift = offsets[k]
            for x in range(tx):
                image[k, x] = image[k, x] + snaps[j, 0, HMAX - shift + x] * snaps[j, 1, HMAX + shift + x]
            return carry

        lax.fori_loop(0, nh, one, 0)

    def block(j, carry):
        for i in range(SNAP):
            p = i % 2
            for r in range(2):
                inject(j * SNAP + i, r)
                advance(p, r)
                if i == 2 and r == 0:
                    @pl.when(j > 0)
                    def _():
                        wait_snap(j - 1)
                        correlate(j - 1)
                wait_halos(p, r)
                repair(p, r, j if i == SNAP - 1 else None)
                if i == SNAP - 1:
                    @pl.when(j < blocks - 1)
                    def _():
                        send_halos(1 - p, r)

                    @pl.when(j == blocks - 1)
                    def _():
                        send_snap(j, r)
                else:
                    send_halos(1 - p, r)
                if i == 0:
                    @pl.when(j > 0)
                    def _():
                        send_snap(j - 1, r)
        return carry

    lax.fori_loop(0, blocks, block, 0)
    wait_snap(blocks - 1)

    def peer_copy(d, arrival=False):
        return pltpu.make_async_remote_copy(
            src_ref=outgoing.at[d], dst_ref=gathered.at[d if arrival else g], send_sem=gs.at[d],
            recv_sem=gr.at[d if arrival else g],
            device_id={"grp": d, "gx": a, "gy": b}, device_id_type=MESH,
        )

    def finish(d, target):
        def pair(n, carry):
            for x in range(tx):
                tiles = []
                for c in range(2):
                    k = d * own + 2 * n + c
                    shift = offsets[k]
                    tile = image[k, x] + snaps[blocks - 1, 0, HMAX - shift + x] * snaps[blocks - 1, 1, HMAX + shift + x]
                    tiles.append(tile + turn(tile, qy))
                target[n, x] = jnp.where(first, tiles[0], tiles[1])
            return carry

        lax.fori_loop(0, own // 2, pair, 0)

    for step in range(1, ng):
        d = (g + step) % ng
        finish(d, outgoing.at[d])
        peer_copy(d).start()
    finish(g, gathered.at[g])
    for step in range(1, ng):
        d = (g + step) % ng
        peer_copy(d, True).wait_recv()
        peer_copy(d).wait_send()


def place(gathered, out):
    ng, pairs, span, sub, nz = gathered.shape
    flip = lax.axis_index("gy") % 2
    qy = sub // 2
    first = lax.broadcasted_iota(jnp.int32, (sub, nz), 0) < qy
    for h in range(ng // 2):
        left, right = 2 * h, 2 * h + 1
        one = left + flip * (ng - 1 - 2 * left)
        two = right + flip * (ng - 1 - 2 * right)
        for n in range(pairs):
            for x in range(span):
                u, v = gathered[one, n, x], gathered[two, n, x]
                out[2 * n, x, pl.ds(h * sub, sub), :] = jnp.where(first, u, pltpu.roll(v, qy, 0))
                out[2 * n + 1, x, pl.ds(h * sub, sub), :] = jnp.where(first, pltpu.roll(u, qy, 0), v)


def shards(sizes, checkpoint, courant, epsilon, delta, positions, amplitudes, offsets):
    ng, nx, ny = sizes
    shots = checkpoint.shape[0]
    tx, ty, nz = courant.shape
    nrec = positions.shape[2]
    blocks = amplitudes.shape[1] // SNAP
    nh = offsets.shape[0]
    own = nh // ng
    qy = ty // ng
    sub = shots * qy
    groups = tx // qy
    assert shots == 2 and sub == 8 and ng % 2 == 0 and own % 2 == 0 and tx % qy == 0 and tx >= HMAX
    f32 = jnp.float32
    dma = pltpu.SemaphoreType.DMA
    vmem = pl.BlockSpec(memory_space=pltpu.VMEM)
    gathered = pl.pallas_call(
        functools.partial(kernel, sizes),
        out_shape=jax.ShapeDtypeStruct((ng, own // 2, tx, sub, nz), f32),
        in_specs=[vmem] * 6 + [pl.BlockSpec(memory_space=pltpu.SMEM)],
        out_specs=vmem,
        scratch_shapes=[
            pltpu.VMEM((2, 2, 2, tx, sub, nz), f32),
            pltpu.VMEM((tx, sub, nz), f32),
            pltpu.VMEM((tx, sub, nz), f32),
            pltpu.VMEM((tx, sub, nz), f32),
            pltpu.VMEM((2, tx * sub, nz), f32),
            pltpu.VMEM((2, tx * sub, shots * nrec), f32),
            pltpu.VMEM((2, shots * nrec, nz), jnp.bfloat16),
            pltpu.VMEM((blocks, 2, tx + 2 * HMAX, sub, nz), f32),
            pltpu.VMEM((nh, tx, sub, nz), f32),
            pltpu.VMEM((ng, own // 2, tx, sub, nz), f32),
            pltpu.VMEM((2, 2, 2, sub, nz), f32),
            pltpu.VMEM((2, 2, 2, groups, sub, nz), f32),
            pltpu.VMEM((2, 2, 2, groups, sub, nz), f32),
            dma((2, 2, 4)),
            dma((2, 2, 4)),
            dma((blocks, 2, 2)),
            dma((blocks, 2, 2)),
            dma((ng,)),
            dma((ng,)),
        ],
        compiler_params=pltpu.CompilerParams(
            collective_id=0, has_side_effects=True, vmem_limit_bytes=56 * 1024 * 1024
        ),
    )(courant, epsilon, delta, checkpoint, positions.transpose(1, 0, 2), amplitudes, offsets)
    cut = math.gcd(tx, 4)
    span = tx // cut
    return pl.pallas_call(
        place,
        grid=(cut,),
        out_shape=jax.ShapeDtypeStruct((own, tx, ty, nz), f32),
        in_specs=[pl.BlockSpec((ng, own // 2, span, sub, nz), lambda n: (0, 0, n, 0, 0))],
        out_specs=pl.BlockSpec((own, span, ty, nz), lambda n: (0, n, 0, 0)),
    )(gathered)


def solution(mesh):
    sizes = tuple(mesh.shape[axis] for axis in ("grp", "gx", "gy"))
    return jax.shard_map(
        functools.partial(shards, sizes),
        mesh=mesh,
        in_specs=(
            P(None, None, None, "gx", "gy", None),
            P("gx", "gy", None),
            P("gx", "gy", None),
            P("gx", "gy", None),
            P(),
            P(),
            P(),
        ),
        out_specs=P("grp", "gx", "gy", None),
        check_vma=False,
    )
```

```python
import functools
import math
import jax
import jax.numpy as jnp
from jax import lax
from jax.experimental import pallas as pl
from jax.experimental.pallas import tpu as pltpu
from jax.sharding import PartitionSpec as P

SNAP = 4
HMAX = 8
MESH = pl.DeviceIdType.MESH


def kernel(sizes, courant, epsilon, delta, checkpoint, positions, amplitudes, offsets, gathered,
           state, hor, cpl, ver, inj, pick, spot, snaps, image, outgoing, hx, hy, sy,
           hs, hr, ss, sr, gs, gr):
    ng, nx, ny = sizes
    shots = checkpoint.shape[0]
    tx, ty, nz = courant.shape
    nrec = positions.shape[2]
    blocks = amplitudes.shape[1] // SNAP
    nh = offsets.shape[0]
    own = nh // ng
    qy = ty // ng
    sub = shots * qy
    groups = tx // qy
    g, a, b = lax.axis_index("grp"), lax.axis_index("gx"), lax.axis_index("gy")
    flip = b % 2
    sign = 1 - 2 * flip
    q = g + flip * (ng - 1 - 2 * g)

    inner_lo, inner_hi = (q > 0).astype(jnp.int32), (q < ng - 1).astype(jnp.int32)
    sides = (
        (a > 0, {"grp": g, "gx": a - 1, "gy": b}),
        (a < nx - 1, {"grp": g, "gx": a + 1, "gy": b}),
        ((q > 0) | (b > 0), {"grp": g - sign * inner_lo, "gx": a, "gy": b - 1 + inner_lo}),
        ((q < ng - 1) | (b < ny - 1), {"grp": g + sign * inner_hi, "gx": a, "gy": b + 1 - inner_hi}),
    )

    barrier = pltpu.get_barrier_semaphore()
    for there, device in sides:
        @pl.when(there)
        def _(device=device):
            pl.semaphore_signal(barrier, inc=1, device_id=device, device_id_type=MESH)
    for step in range(1, ng):
        pl.semaphore_signal(
            barrier, inc=1, device_id={"grp": (g + step) % ng, "gx": a, "gy": b}, device_id_type=MESH
        )

    rows = lax.broadcasted_iota(jnp.int32, (sub, nz), 0)
    lanes = lax.broadcasted_iota(jnp.int32, (sub, nz), 1)
    place = rows % qy
    is_odd = rows * 0 + q % 2 == 1
    first = rows < qy
    half = pl.ds(pl.multiple_of((q // 2) * sub, sub), sub)

    def turn(v, shift, axis=0):
        shift = shift % v.shape[axis]
        return v if shift == 0 else pltpu.roll(v, shift, axis)

    def low(v):
        return jnp.where(is_odd, turn(v, qy), v)

    def high(v):
        return jnp.where(is_odd, v, turn(v, qy))

    def both(v):
        return jnp.where(first, low(v), high(v))

    zero = jnp.zeros((sub, nz), jnp.float32)

    def prepare(x, carry):
        c, e, d = both(courant[x, half, :]), both(epsilon[x, half, :]), both(delta[x, half, :])
        hor[x] = c + 2.0 * c * e
        cpl[x] = c * jnp.sqrt(2.0 * d + 1.0)
        ver[x] = c
        for moment in range(2):
            for field in range(2):
                state[moment, field, 0, x] = jnp.where(
                    first, low(checkpoint[0, moment, field, x, half, :]), high(checkpoint[1, moment, field, x, half, :])
                )
                state[moment, field, 1, x] = zero
        return carry

    lax.fori_loop(0, tx, prepare, 0)

    def pack(side, r, slot, source):
        for m in range(groups):
            packed = None
            for i in range(qy):
                tile = turn(source(m * qy + i), i if side == 0 else i - (qy - 1))
                packed = tile if packed is None else jnp.where(place == i, tile, packed)
            sy[slot, side, r, m] = packed

    for r in range(2):
        for side in range(2):
            pack(side, r, 0, lambda x: state[0, 0, r, x])

    for side in range(2):
        for slot in range(2):
            @pl.when(jnp.logical_not(sides[side][0]))
            def _(slot=slot, side=side):
                hx[slot, side] = jnp.zeros(hx.shape[2:], jnp.float32)

            @pl.when(jnp.logical_not(sides[2 + side][0]))
            def _(slot=slot, side=side):
                hy[slot, side] = jnp.zeros(hy.shape[2:], jnp.float32)

    total = ng - 1
    for there, _ in sides:
        total = total + there.astype(jnp.int32)
    pl.semaphore_wait(barrier, total)

    def halo_copy(slot, r, side):
        if side < 2:
            source, target = state.at[slot, 0, r, 0 if side == 0 else tx - 1], hx.at[slot, 1 - side, r]
        else:
            source, target = sy.at[slot, side - 2, r], hy.at[slot, 3 - side, r]
        return pltpu.make_async_remote_copy(
            src_ref=source, dst_ref=target, send_sem=hs.at[slot, r, side], recv_sem=hr.at[slot, r, side ^ 1],
            device_id=sides[side][1], device_id_type=MESH,
        )

    def halo_arrival(slot, r, side):
        target = hx.at[slot, side, r] if side < 2 else hy.at[slot, side - 2, r]
        return pltpu.make_async_remote_copy(
            src_ref=target, dst_ref=target, send_sem=hs.at[slot, r, side], recv_sem=hr.at[slot, r, side],
            device_id=sides[side][1], device_id_type=MESH,
        )

    def snap_copy(j, r, side, arrival=False):
        source = pl.ds(HMAX, HMAX) if side == 0 else pl.ds(tx, HMAX)
        target = pl.ds(HMAX + tx, HMAX) if side == 0 else pl.ds(0, HMAX)
        if arrival:
            source = target = pl.ds(0, HMAX) if side == 0 else pl.ds(HMAX + tx, HMAX)
        return pltpu.make_async_remote_copy(
            src_ref=snaps.at[j, r, source], dst_ref=snaps.at[j, r, target], send_sem=ss.at[j, r, side],
            recv_sem=sr.at[j, r, side if arrival else side ^ 1], device_id=sides[side][1], device_id_type=MESH,
        )

    def send_halos(slot, r):
        for side in (2, 3, 0, 1):
            @pl.when(sides[side][0])
            def _(side=side):
                halo_copy(slot, r, side).start()

    def wait_halos(slot, r):
        for side in range(4):
            @pl.when(sides[side][0])
            def _(side=side):
                halo_arrival(slot, r, side).wait_recv()
                halo_copy(slot, r, side).wait_send()

    def send_snap(j, r):
        for side in range(2):
            @pl.when(sides[side][0])
            def _(side=side):
                snap_copy(j, r, side).start()

    def wait_snap(j):
        for r in range(2):
            for side in range(2):
                @pl.when(sides[side][0])
                def _(r=r, side=side):
                    snap_copy(j, r, side, True).wait_recv()
                    snap_copy(j, r, side).wait_send()

    send_halos(0, 0)
    send_halos(0, 1)

    column = lax.broadcasted_iota(jnp.int32, (tx * sub, nrec), 0)
    level = lax.broadcasted_iota(jnp.int32, (nz, nrec), 0)
    for r in range(2):
        for s in range(shots):
            px = positions[0, 2 * s + r : 2 * s + r + 1, :] - a * tx
            py = positions[1, 2 * s + r : 2 * s + r + 1, :] - (b * ty + q * qy)
            pz = positions[2, 2 * s + r : 2 * s + r + 1, :]
            inside = (px >= 0) & (px < tx) & (py >= 0) & (py < qy)
            cell = jnp.where(inside, px * sub + s * qy + py, -1)
            points = pl.ds(s * nrec, nrec)
            pick[r, :, points] = jnp.where(column == cell, 1.0, 0.0).astype(jnp.bfloat16)
            spot[r, points, :] = jnp.where(level == pz, 1.0, 0.0).T.astype(jnp.bfloat16)

    def clear(k, carry):
        for x in range(tx):
            image[k, x] = zero
        return carry

    lax.fori_loop(0, nh, clear, 0)
    for side in range(2):
        @pl.when(jnp.logical_not(sides[side][0]))
        def _(side=side):
            def blank(j, carry):
                for r in range(2):
                    for x in range(HMAX):
                        snaps[j, r, side * (HMAX + tx) + x] = zero
                return carry

            lax.fori_loop(0, blocks, blank, 0)

    def inject(moment, r):
        strength = jnp.concatenate(
            [amplitudes[2 * s + r, pl.ds(moment, 1), :] for s in range(shots)], axis=1
        )
        strength = jnp.broadcast_to(strength, (2 * sub, shots * nrec))
        upper = strength.astype(jnp.bfloat16)
        lower = (strength - upper.astype(jnp.float32)).astype(jnp.bfloat16)
        spread = jnp.concatenate(
            [
                pick[r, pl.ds(2 * sub * m, 2 * sub), :] * part
                for part in (upper, lower)
                for m in range(tx // 2)
            ],
            axis=0,
        )
        found = jnp.dot(spread, spot[r], preferred_element_type=jnp.float32)
        inj[r] = found[: tx * sub] + found[tx * sub :]

    def advance(p, r):
        for x in range(tx):
            m, w = state[p, 0, r, x], state[p, 1, r, x]
            across = (
                jnp.where(place == 0, 0.0, turn(m, 1))
                + jnp.where(place == qy - 1, 0.0, turn(m, -1))
                - 4.0 * m
            )
            if x > 0:
                across = across + state[p, 0, r, x - 1]
            if x < tx - 1:
                across = across + state[p, 0, r, x + 1]
            down = (
                jnp.where(lanes == 0, 0.0, turn(w, 1, 1))
                + jnp.where(lanes == nz - 1, 0.0, turn(w, -1, 1))
                - 2.0 * w
            )
            source = inj[r, pl.ds(x * sub, sub), :]
            coupling = cpl[x]
            state[1 - p, 0, r, x] = 2.0 * m - state[1 - p, 0, r, x] + hor[x] * across + coupling * down + source
            state[1 - p, 1, r, x] = 2.0 * w - state[1 - p, 1, r, x] + coupling * across + ver[x] * down + source

    def repair(p, r, j):
        for m in range(groups):
            below, above = hy[p, 0, r, m], hy[p, 1, r, m]
            packed = [None, None]
            for i in range(qy):
                x = m * qy + i
                extra = jnp.where(place == 0, turn(below, -i), 0.0)
                extra = jnp.where(place == qy - 1, turn(above, qy - 1 - i), extra)
                if x == 0:
                    extra = extra + hx[p, 0, r]
                if x == tx - 1:
                    extra = extra + hx[p, 1, r]
                main = state[1 - p, 0, r, x] + hor[x] * extra
                state[1 - p, 0, r, x] = main
                state[1 - p, 1, r, x] = state[1 - p, 1, r, x] + cpl[x] * extra
                for side in range(2):
                    tile = turn(main, i if side == 0 else i - (qy - 1))
                    packed[side] = tile if i == 0 else jnp.where(place == i, tile, packed[side])
                if j is not None:
                    snaps[j, r, HMAX + x] = main
            for side in range(2):
                sy[1 - p, side, r, m] = packed[side]

    def correlate(j):
        def one(k, carry):
            shift = offsets[k]
            for x in range(tx):
                image[k, x] = image[k, x] + snaps[j, 0, HMAX - shift + x] * snaps[j, 1, HMAX + shift + x]
            return carry

        lax.fori_loop(0, nh, one, 0)

    def block(j, carry):
        for i in range(SNAP):
            p = i % 2
            for r in range(2):
                inject(j * SNAP + i, r)
                advance(p, r)
                if i == 2 and r == 0:
                    @pl.when(j > 0)
                    def _():
                        wait_snap(j - 1)
                        correlate(j - 1)
                wait_halos(p, r)
                repair(p, r, j if i == SNAP - 1 else None)
                if i == SNAP - 1:
                    @pl.when(j < blocks - 1)
                    def _():
                        send_halos(1 - p, r)

                    @pl.when(j == blocks - 1)
                    def _():
                        send_snap(j, r)
                else:
                    send_halos(1 - p, r)
                if i == 0:
                    @pl.when(j > 0)
                    def _():
                        send_snap(j - 1, r)
        return carry

    lax.fori_loop(0, blocks, block, 0)
    wait_snap(blocks - 1)

    def peer_copy(d, arrival=False):
        return pltpu.make_async_remote_copy(
            src_ref=outgoing.at[d], dst_ref=gathered.at[d if arrival else g], send_sem=gs.at[d],
            recv_sem=gr.at[d if arrival else g],
            device_id={"grp": d, "gx": a, "gy": b}, device_id_type=MESH,
        )

    def finish(d, target):
        def pair(n, carry):
            for x in range(tx):
                tiles = []
                for c in range(2):
                    k = d * own + 2 * n + c
                    shift = offsets[k]
                    tile = image[k, x] + snaps[blocks - 1, 0, HMAX - shift + x] * snaps[blocks - 1, 1, HMAX + shift + x]
                    tiles.append(tile + turn(tile, qy))
                target[n, x] = jnp.where(first, tiles[0], tiles[1])
            return carry

        lax.fori_loop(0, own // 2, pair, 0)

    for step in range(1, ng):
        d = (g + step) % ng
        finish(d, outgoing.at[d])
        peer_copy(d).start()
    finish(g, gathered.at[g])
    for step in range(1, ng):
        d = (g + step) % ng
        peer_copy(d, True).wait_recv()
        peer_copy(d).wait_send()


def place(gathered, out):
    ng, pairs, span, sub, nz = gathered.shape
    flip = lax.axis_index("gy") % 2
    qy = sub // 2
    first = lax.broadcasted_iota(jnp.int32, (sub, nz), 0) < qy
    for h in range(ng // 2):
        left, right = 2 * h, 2 * h + 1
        one = left + flip * (ng - 1 - 2 * left)
        two = right + flip * (ng - 1 - 2 * right)
        for n in range(pairs):
            for x in range(span):
                u, v = gathered[one, n, x], gathered[two, n, x]
                out[2 * n, x, pl.ds(h * sub, sub), :] = jnp.where(first, u, pltpu.roll(v, qy, 0))
                out[2 * n + 1, x, pl.ds(h * sub, sub), :] = jnp.where(first, pltpu.roll(u, qy, 0), v)


def shards(sizes, checkpoint, courant, epsilon, delta, positions, amplitudes, offsets):
    ng, nx, ny = sizes
    shots = checkpoint.shape[0]
    tx, ty, nz = courant.shape
    nrec = positions.shape[2]
    blocks = amplitudes.shape[1] // SNAP
    nh = offsets.shape[0]
    own = nh // ng
    qy = ty // ng
    sub = shots * qy
    groups = tx // qy
    assert shots == 2 and sub == 8 and ng % 2 == 0 and own % 2 == 0 and tx % qy == 0 and tx >= HMAX and tx % 2 == 0
    f32 = jnp.float32
    dma = pltpu.SemaphoreType.DMA
    vmem = pl.BlockSpec(memory_space=pltpu.VMEM)
    gathered = pl.pallas_call(
        functools.partial(kernel, sizes),
        out_shape=jax.ShapeDtypeStruct((ng, own // 2, tx, sub, nz), f32),
        in_specs=[vmem] * 6 + [pl.BlockSpec(memory_space=pltpu.SMEM)],
        out_specs=vmem,
        scratch_shapes=[
            pltpu.VMEM((2, 2, 2, tx, sub, nz), f32),
            pltpu.VMEM((tx, sub, nz), f32),
            pltpu.VMEM((tx, sub, nz), f32),
            pltpu.VMEM((tx, sub, nz), f32),
            pltpu.VMEM((2, tx * sub, nz), f32),
            pltpu.VMEM((2, tx * sub, shots * nrec), jnp.bfloat16),
            pltpu.VMEM((2, shots * nrec, nz), jnp.bfloat16),
            pltpu.VMEM((blocks, 2, tx + 2 * HMAX, sub, nz), f32),
            pltpu.VMEM((nh, tx, sub, nz), f32),
            pltpu.VMEM((ng, own // 2, tx, sub, nz), f32),
            pltpu.VMEM((2, 2, 2, sub, nz), f32),
            pltpu.VMEM((2, 2, 2, groups, sub, nz), f32),
            pltpu.VMEM((2, 2, 2, groups, sub, nz), f32),
            dma((2, 2, 4)),
            dma((2, 2, 4)),
            dma((blocks, 2, 2)),
            dma((blocks, 2, 2)),
            dma((ng,)),
            dma((ng,)),
        ],
        compiler_params=pltpu.CompilerParams(
            collective_id=0, has_side_effects=True, vmem_limit_bytes=56 * 1024 * 1024
        ),
    )(courant, epsilon, delta, checkpoint, positions.transpose(1, 0, 2), amplitudes, offsets)
    cut = math.gcd(tx, 4)
    span = tx // cut
    return pl.pallas_call(
        place,
        grid=(cut,),
        out_shape=jax.ShapeDtypeStruct((own, tx, ty, nz), f32),
        in_specs=[pl.BlockSpec((ng, own // 2, span, sub, nz), lambda n: (0, 0, n, 0, 0))],
        out_specs=pl.BlockSpec((own, span, ty, nz), lambda n: (0, n, 0, 0)),
    )(gathered)


def solution(mesh):
    sizes = tuple(mesh.shape[axis] for axis in ("grp", "gx", "gy"))
    return jax.shard_map(
        functools.partial(shards, sizes),
        mesh=mesh,
        in_specs=(
            P(None, None, None, "gx", "gy", None),
            P("gx", "gy", None),
            P("gx", "gy", None),
            P("gx", "gy", None),
            P(),
            P(),
            P(),
        ),
        out_specs=P("grp", "gx", "gy", None),
        check_vma=False,
    )
```

```python
import functools
import math
import jax
import jax.numpy as jnp
from jax import lax
from jax.experimental import pallas as pl
from jax.experimental.pallas import tpu as pltpu
from jax.sharding import PartitionSpec as P

SNAP = 4
HMAX = 8
MESH = pl.DeviceIdType.MESH


def kernel(sizes, courant, epsilon, delta, checkpoint, positions, amplitudes, offsets, gathered,
           state, hor, cpl, ver, edge, inj, pick, spot, snaps, image, outgoing, hx, hy, sy,
           hs, hr, ss, sr, gs, gr):
    ng, nx, ny = sizes
    shots = checkpoint.shape[0]
    tx, ty, nz = courant.shape
    nrec = positions.shape[2]
    blocks = amplitudes.shape[1] // SNAP
    nh = offsets.shape[0]
    own = nh // ng
    qy = ty // ng
    sub = shots * qy
    groups = tx // qy
    g, a, b = lax.axis_index("grp"), lax.axis_index("gx"), lax.axis_index("gy")
    flip = b % 2
    sign = 1 - 2 * flip
    q = g + flip * (ng - 1 - 2 * g)

    inner_lo, inner_hi = (q > 0).astype(jnp.int32), (q < ng - 1).astype(jnp.int32)
    sides = (
        (a > 0, {"grp": g, "gx": a - 1, "gy": b}),
        (a < nx - 1, {"grp": g, "gx": a + 1, "gy": b}),
        ((q > 0) | (b > 0), {"grp": g - sign * inner_lo, "gx": a, "gy": b - 1 + inner_lo}),
        ((q < ng - 1) | (b < ny - 1), {"grp": g + sign * inner_hi, "gx": a, "gy": b + 1 - inner_hi}),
    )

    barrier = pltpu.get_barrier_semaphore()
    for there, device in sides:
        @pl.when(there)
        def _(device=device):
            pl.semaphore_signal(barrier, inc=1, device_id=device, device_id_type=MESH)
    for step in range(1, ng):
        pl.semaphore_signal(
            barrier, inc=1, device_id={"grp": (g + step) % ng, "gx": a, "gy": b}, device_id_type=MESH
        )

    rows = lax.broadcasted_iota(jnp.int32, (sub, nz), 0)
    lanes = lax.broadcasted_iota(jnp.int32, (sub, nz), 1)
    place = rows % qy
    is_odd = rows * 0 + q % 2 == 1
    first = rows < qy
    half = pl.ds(pl.multiple_of((q // 2) * sub, sub), sub)

    def turn(v, shift, axis=0):
        shift = shift % v.shape[axis]
        return v if shift == 0 else pltpu.roll(v, shift, axis)

    def low(v):
        return jnp.where(is_odd, turn(v, qy), v)

    def high(v):
        return jnp.where(is_odd, v, turn(v, qy))

    def both(v):
        return jnp.where(first, low(v), high(v))

    zero = jnp.zeros((sub, nz), jnp.float32)

    def prepare(x, carry):
        c, e, d = both(courant[x, half, :]), both(epsilon[x, half, :]), both(delta[x, half, :])
        hor[x] = c + 2.0 * c * e
        cpl[x] = c * jnp.sqrt(2.0 * d + 1.0)
        ver[x] = c
        for moment in range(2):
            for field in range(2):
                state[moment, field, 0, x] = jnp.where(
                    first, low(checkpoint[0, moment, field, x, half, :]), high(checkpoint[1, moment, field, x, half, :])
                )
                state[moment, field, 1, x] = zero
        return carry

    lax.fori_loop(0, tx, prepare, 0)

    def pack(side, r, slot, source):
        for m in range(groups):
            packed = None
            for i in range(qy):
                tile = turn(source(m * qy + i), i if side == 0 else i - (qy - 1))
                packed = tile if packed is None else jnp.where(place == i, tile, packed)
            sy[slot, side, r, m] = packed

    for r in range(2):
        for side in range(2):
            pack(side, r, 0, lambda x: state[0, 0, r, x])

    for side in range(2):
        for slot in range(2):
            @pl.when(jnp.logical_not(sides[side][0]))
            def _(slot=slot, side=side):
                hx[slot, side] = jnp.zeros(hx.shape[2:], jnp.float32)

            @pl.when(jnp.logical_not(sides[2 + side][0]))
            def _(slot=slot, side=side):
                hy[slot, side] = jnp.zeros(hy.shape[2:], jnp.float32)

    total = ng - 1
    for there, _ in sides:
        total = total + there.astype(jnp.int32)
    pl.semaphore_wait(barrier, total)

    def halo_copy(slot, r, side):
        if side < 2:
            source, target = state.at[slot, 0, r, 0 if side == 0 else tx - 1], hx.at[slot, 1 - side, r]
        else:
            source, target = sy.at[slot, side - 2, r], hy.at[slot, 3 - side, r]
        return pltpu.make_async_remote_copy(
            src_ref=source, dst_ref=target, send_sem=hs.at[slot, r, side], recv_sem=hr.at[slot, r, side ^ 1],
            device_id=sides[side][1], device_id_type=MESH,
        )

    def halo_arrival(slot, r, side):
        target = hx.at[slot, side, r] if side < 2 else hy.at[slot, side - 2, r]
        return pltpu.make_async_remote_copy(
            src_ref=target, dst_ref=target, send_sem=hs.at[slot, r, side], recv_sem=hr.at[slot, r, side],
            device_id=sides[side][1], device_id_type=MESH,
        )

    def snap_copy(j, r, side, arrival=False):
        source = pl.ds(HMAX, HMAX) if side == 0 else pl.ds(tx, HMAX)
        target = pl.ds(HMAX + tx, HMAX) if side == 0 else pl.ds(0, HMAX)
        if arrival:
            source = target = pl.ds(0, HMAX) if side == 0 else pl.ds(HMAX + tx, HMAX)
        return pltpu.make_async_remote_copy(
            src_ref=snaps.at[j, r, source], dst_ref=snaps.at[j, r, target], send_sem=ss.at[j, r, side],
            recv_sem=sr.at[j, r, side if arrival else side ^ 1], device_id=sides[side][1], device_id_type=MESH,
        )

    def send_halos(slot, r):
        for side in (2, 3, 0, 1):
            @pl.when(sides[side][0])
            def _(side=side):
                halo_copy(slot, r, side).start()

    def wait_halos(slot, r):
        for side in range(4):
            @pl.when(sides[side][0])
            def _(side=side):
                halo_arrival(slot, r, side).wait_recv()
                halo_copy(slot, r, side).wait_send()

    def send_snap(j, r):
        for side in range(2):
            @pl.when(sides[side][0])
            def _(side=side):
                snap_copy(j, r, side).start()

    def wait_snap(j):
        for r in range(2):
            for side in range(2):
                @pl.when(sides[side][0])
                def _(r=r, side=side):
                    snap_copy(j, r, side, True).wait_recv()
                    snap_copy(j, r, side).wait_send()

    send_halos(0, 0)
    send_halos(0, 1)

    column = lax.broadcasted_iota(jnp.int32, (tx * sub, nrec), 0)
    level = lax.broadcasted_iota(jnp.int32, (nz, nrec), 0)
    for r in range(2):
        for s in range(shots):
            px = positions[0, 2 * s + r : 2 * s + r + 1, :] - a * tx
            py = positions[1, 2 * s + r : 2 * s + r + 1, :] - (b * ty + q * qy)
            pz = positions[2, 2 * s + r : 2 * s + r + 1, :]
            inside = (px >= 0) & (px < tx) & (py >= 0) & (py < qy)
            cell = jnp.where(inside, px * sub + s * qy + py, -1)
            points = pl.ds(s * nrec, nrec)
            pick[r, :, points] = jnp.where(column == cell, 1.0, 0.0).astype(jnp.bfloat16)
            spot[r, points, :] = jnp.where(level == pz, 1.0, 0.0).T.astype(jnp.bfloat16)

    def clear(k, carry):
        for x in range(tx):
            image[k, x] = zero
        return carry

    lax.fori_loop(0, nh, clear, 0)
    for side in range(2):
        @pl.when(jnp.logical_not(sides[side][0]))
        def _(side=side):
            def blank(j, carry):
                for r in range(2):
                    for x in range(HMAX):
                        snaps[j, r, side * (HMAX + tx) + x] = zero
                return carry

            lax.fori_loop(0, blocks, blank, 0)

    def inject(moment, r):
        strength = jnp.concatenate(
            [amplitudes[2 * s + r, pl.ds(moment, 1), :] for s in range(shots)], axis=1
        )
        strength = jnp.broadcast_to(strength, (2 * sub, shots * nrec))
        upper = strength.astype(jnp.bfloat16)
        lower = (strength - upper.astype(jnp.float32)).astype(jnp.bfloat16)
        spread = jnp.concatenate(
            [
                pick[r, pl.ds(2 * sub * m, 2 * sub), :] * part
                for part in (upper, lower)
                for m in range(tx // 2)
            ],
            axis=0,
        )
        found = jnp.dot(spread, spot[r], preferred_element_type=jnp.float32)
        inj[r] = found[: tx * sub] + found[tx * sub :]

    def advance(p, r):
        for x in range(tx):
            m, w = state[p, 0, r, x], state[p, 1, r, x]
            across = (
                jnp.where(place == 0, 0.0, turn(m, 1))
                + jnp.where(place == qy - 1, 0.0, turn(m, -1))
                - 4.0 * m
            )
            if x > 0:
                across = across + state[p, 0, r, x - 1]
            if x < tx - 1:
                across = across + state[p, 0, r, x + 1]
            down = (
                jnp.where(lanes == 0, 0.0, turn(w, 1, 1))
                + jnp.where(lanes == nz - 1, 0.0, turn(w, -1, 1))
                - 2.0 * w
            )
            source = inj[r, pl.ds(x * sub, sub), :]
            coupling = cpl[x]
            state[1 - p, 0, r, x] = 2.0 * m - state[1 - p, 0, r, x] + hor[x] * across + coupling * down + source
            state[1 - p, 1, r, x] = 2.0 * w - state[1 - p, 1, r, x] + coupling * across + ver[x] * down + source

    def repair(p, r, j):
        for m in range(groups):
            below, above = hy[p, 0, r, m], hy[p, 1, r, m]
            packed = [None, None]
            for i in range(qy):
                x = m * qy + i
                extra = jnp.where(place == 0, turn(below, -i), 0.0)
                extra = jnp.where(place == qy - 1, turn(above, qy - 1 - i), extra)
                if x == 0:
                    extra = extra + hx[p, 0, r]
                if x == tx - 1:
                    extra = extra + hx[p, 1, r]
                main = state[1 - p, 0, r, x] + hor[x] * extra
                state[1 - p, 0, r, x] = main
                edge[x] = extra
                for side in range(2):
                    tile = turn(main, i if side == 0 else i - (qy - 1))
                    packed[side] = tile if i == 0 else jnp.where(place == i, tile, packed[side])
                if j is not None:
                    snaps[j, r, HMAX + x] = main
            for side in range(2):
                sy[1 - p, side, r, m] = packed[side]

    def repair_aux(p, r):
        for x in range(tx):
            state[1 - p, 1, r, x] = state[1 - p, 1, r, x] + cpl[x] * edge[x]

    def correlate(j):
        def one(k, carry):
            shift = offsets[k]
            for x in range(tx):
                image[k, x] = image[k, x] + snaps[j, 0, HMAX - shift + x] * snaps[j, 1, HMAX + shift + x]
            return carry

        lax.fori_loop(0, nh, one, 0)

    def block(j, carry):
        for i in range(SNAP):
            p = i % 2
            for r in range(2):
                inject(j * SNAP + i, r)
                advance(p, r)
                if i == 2 and r == 0:
                    @pl.when(j > 0)
                    def _():
                        wait_snap(j - 1)
                        correlate(j - 1)
                wait_halos(p, r)
                repair(p, r, j if i == SNAP - 1 else None)
                if i == SNAP - 1:
                    @pl.when(j < blocks - 1)
                    def _():
                        send_halos(1 - p, r)

                    @pl.when(j == blocks - 1)
                    def _():
                        send_snap(j, r)
                else:
                    send_halos(1 - p, r)
                if i == 0:
                    @pl.when(j > 0)
                    def _():
                        send_snap(j - 1, r)
                repair_aux(p, r)
        return carry

    lax.fori_loop(0, blocks, block, 0)
    wait_snap(blocks - 1)

    def peer_copy(d, arrival=False):
        return pltpu.make_async_remote_copy(
            src_ref=outgoing.at[d], dst_ref=gathered.at[d if arrival else g], send_sem=gs.at[d],
            recv_sem=gr.at[d if arrival else g],
            device_id={"grp": d, "gx": a, "gy": b}, device_id_type=MESH,
        )

    def finish(d, target):
        def pair(n, carry):
            for x in range(tx):
                tiles = []
                for c in range(2):
                    k = d * own + 2 * n + c
                    shift = offsets[k]
                    tile = image[k, x] + snaps[blocks - 1, 0, HMAX - shift + x] * snaps[blocks - 1, 1, HMAX + shift + x]
                    tiles.append(tile + turn(tile, qy))
                target[n, x] = jnp.where(first, tiles[0], tiles[1])
            return carry

        lax.fori_loop(0, own // 2, pair, 0)

    for step in range(1, ng):
        d = (g + step) % ng
        finish(d, outgoing.at[d])
        peer_copy(d).start()
    finish(g, gathered.at[g])
    for step in range(1, ng):
        d = (g + step) % ng
        peer_copy(d, True).wait_recv()
        peer_copy(d).wait_send()


def place(gathered, out):
    ng, pairs, span, sub, nz = gathered.shape
    flip = lax.axis_index("gy") % 2
    qy = sub // 2
    first = lax.broadcasted_iota(jnp.int32, (sub, nz), 0) < qy
    for h in range(ng // 2):
        left, right = 2 * h, 2 * h + 1
        one = left + flip * (ng - 1 - 2 * left)
        two = right + flip * (ng - 1 - 2 * right)
        for n in range(pairs):
            for x in range(span):
                u, v = gathered[one, n, x], gathered[two, n, x]
                out[2 * n, x, pl.ds(h * sub, sub), :] = jnp.where(first, u, pltpu.roll(v, qy, 0))
                out[2 * n + 1, x, pl.ds(h * sub, sub), :] = jnp.where(first, pltpu.roll(u, qy, 0), v)


def shards(sizes, checkpoint, courant, epsilon, delta, positions, amplitudes, offsets):
    ng, nx, ny = sizes
    shots = checkpoint.shape[0]
    tx, ty, nz = courant.shape
    nrec = positions.shape[2]
    blocks = amplitudes.shape[1] // SNAP
    nh = offsets.shape[0]
    own = nh // ng
    qy = ty // ng
    sub = shots * qy
    groups = tx // qy
    assert shots == 2 and sub == 8 and ng % 2 == 0 and own % 2 == 0 and tx % qy == 0 and tx >= HMAX and tx % 2 == 0
    f32 = jnp.float32
    dma = pltpu.SemaphoreType.DMA
    vmem = pl.BlockSpec(memory_space=pltpu.VMEM)
    gathered = pl.pallas_call(
        functools.partial(kernel, sizes),
        out_shape=jax.ShapeDtypeStruct((ng, own // 2, tx, sub, nz), f32),
        in_specs=[vmem] * 6 + [pl.BlockSpec(memory_space=pltpu.SMEM)],
        out_specs=vmem,
        scratch_shapes=[
            pltpu.VMEM((2, 2, 2, tx, sub, nz), f32),
            pltpu.VMEM((tx, sub, nz), f32),
            pltpu.VMEM((tx, sub, nz), f32),
            pltpu.VMEM((tx, sub, nz), f32),
            pltpu.VMEM((tx, sub, nz), f32),
            pltpu.VMEM((2, tx * sub, nz), f32),
            pltpu.VMEM((2, tx * sub, shots * nrec), jnp.bfloat16),
            pltpu.VMEM((2, shots * nrec, nz), jnp.bfloat16),
            pltpu.VMEM((blocks, 2, tx + 2 * HMAX, sub, nz), f32),
            pltpu.VMEM((nh, tx, sub, nz), f32),
            pltpu.VMEM((ng, own // 2, tx, sub, nz), f32),
            pltpu.VMEM((2, 2, 2, sub, nz), f32),
            pltpu.VMEM((2, 2, 2, groups, sub, nz), f32),
            pltpu.VMEM((2, 2, 2, groups, sub, nz), f32),
            dma((2, 2, 4)),
            dma((2, 2, 4)),
            dma((blocks, 2, 2)),
            dma((blocks, 2, 2)),
            dma((ng,)),
            dma((ng,)),
        ],
        compiler_params=pltpu.CompilerParams(
            collective_id=0, has_side_effects=True, vmem_limit_bytes=56 * 1024 * 1024
        ),
    )(courant, epsilon, delta, checkpoint, positions.transpose(1, 0, 2), amplitudes, offsets)
    cut = math.gcd(tx, 4)
    span = tx // cut
    return pl.pallas_call(
        place,
        grid=(cut,),
        out_shape=jax.ShapeDtypeStruct((own, tx, ty, nz), f32),
        in_specs=[pl.BlockSpec((ng, own // 2, span, sub, nz), lambda n: (0, 0, n, 0, 0))],
        out_specs=pl.BlockSpec((own, span, ty, nz), lambda n: (0, n, 0, 0)),
    )(gathered)


def solution(mesh):
    sizes = tuple(mesh.shape[axis] for axis in ("grp", "gx", "gy"))
    return jax.shard_map(
        functools.partial(shards, sizes),
        mesh=mesh,
        in_specs=(
            P(None, None, None, "gx", "gy", None),
            P("gx", "gy", None),
            P("gx", "gy", None),
            P("gx", "gy", None),
            P(),
            P(),
            P(),
        ),
        out_specs=P("grp", "gx", "gy", None),
        check_vma=False,
    )
```
